32 devices in a mesh: groups: 2 (over y), feat: 4 (over z), tok: 2 (over x), rep: 2 (over core).
Axes of the slice: x: 2, y: 2, z: 4, core: 2. Of those that a mesh axis runs over, the one named last changes fastest.
Arguments:
- tokens: bfloat16 [448, 8192], P(('groups', 'tok', 'rep'), 'feat'), parts along dimension 0, may hold values from -6 to 6
- gate_weight: bfloat16 [8192, 14336], P('feat', ('tok', 'rep')), may hold values from -0.09375 to 0.09375
- up_weight: bfloat16 [8192, 14336], P('feat', ('tok', 'rep')), may hold values from -0.09375 to 0.09375
- down_weight: bfloat16 [14336, 8192], P(('tok', 'rep'), 'feat'), may hold values from -0.0625 to 0.0625
- gate_mask: int32 [64, 112], P('feat', ('tok', 'rep')), may hold values 0 or 1
- up_mask: int32 [64, 112], P('feat', ('tok', 'rep')), may hold values 0 or 1
- down_mask: int32 [112, 64], P(('tok', 'rep'), 'feat'), may hold values 0 or 1
Outputs:
- mixed: bfloat16 [448, 8192], P(('groups', 'tok', 'rep'), 'feat'), parts along dimension 0
The draws below stay inside these ranges and needn't reach their ends.
There are 2 independent parts, one for each index of `groups`. The reference program is written for one: setup_inputs(seed, part) draws one part's arguments, and reference() takes and returns one part's arrays. A program takes and returns all parts, laid end to end along the dimension named above; an argument that names none is the same for every part. Nothing has to cross between parts.
Inputs may be any that keep to these rules, and one draw needn't show every extreme that they name: `gate_mask`: entries are 0 or 1; 1 keeps the block. `up_mask`: entries are 0 or 1; 1 keeps the block. `down_mask`: entries are 0 or 1; 1 keeps the block.
All inputs are finite; a program needn't handle non-finite values.
Results may differ from the reference program's by a relative error of at most 0.02.
Values may be sent and summed in bfloat16 or wider, within the bound.
A program may use at most 192 MiB of HBM per device.

```python
import jax
import jax.numpy as jnp
from jax import lax

D = 8192
HID = 14336
BLOCK = 128
TOKENS = 224
N_FEAT = 4
N_TOK = 2
N_REP = 2


def plant(array, own_key, low, top_value):
    spot = [jax.random.randint(jax.random.fold_in(own_key, axis), (), 0, length) for axis, length in enumerate(array.shape)]
    main_axis = array.shape.index(max(array.shape))
    beside = spot[:main_axis] + [(spot[main_axis] + 1) % array.shape[main_axis]] + spot[main_axis + 1:]
    return array.at[tuple(spot)].set(low).at[tuple(beside)].set(top_value)


def shard_levels(key, extent, shards, least, high):
    def one(axis_at, parts):
        steps = jax.random.uniform(jax.random.fold_in(jax.random.fold_in(key, 6), axis_at), (parts,), jnp.float32, least / len(shards), high / len(shards))
        return jnp.repeat(jnp.exp(steps), extent[axis_at] // parts).reshape((-1,) + (1,) * (len(extent) - axis_at - 1))

    loudness = one(*shards[0])
    for cut in shards[1:]:
        loudness = loudness * one(*cut)
    return loudness


def noise(rng, extent, deviation, limit, shards=(), dtype=jnp.bfloat16):
    gain = shard_levels(rng, extent, shards, -0.22, 0.18) if shards else 1.0
    entries = jax.random.normal(rng, extent, jnp.float32) * deviation * gain
    return jnp.minimum(jnp.maximum(entries, -limit), limit).astype(dtype)


def setup_inputs(seed: int = 0, part: int = 0) -> dict:
    seeds = jax.random.split(jax.random.key(seed), 8)
    part_splits = jax.random.split(jax.random.fold_in(seeds[7], part), 8)
    return {
        "tokens": noise(part_splits[0], (TOKENS, D), 1.0, 6.0, ((0, 4), (1, 4))),
        "gate_weight": noise(seeds[1], (D, HID), (D // 2) ** -0.5, 0.09375, ((0, 4), (1, 4))),
        "up_weight": noise(seeds[2], (D, HID), (D // 2) ** -0.5, 0.09375, ((0, 4), (1, 4))),
        "down_weight": noise(seeds[3], (HID, D), (HID // 2) ** -0.5, 0.0625, ((0, 4), (1, 4))),
        "gate_mask": plant((jax.random.randint(seeds[4], (D // BLOCK, HID // BLOCK), 0, 2) < 1).astype(jnp.int32), jax.random.fold_in(seeds[4], 1), 0, 1),
        "up_mask": plant((jax.random.randint(seeds[5], (D // BLOCK, HID // BLOCK), 0, 2) < 1).astype(jnp.int32), jax.random.fold_in(seeds[5], 1), 0, 1),
        "down_mask": plant((jax.random.randint(seeds[6], (HID // BLOCK, D // BLOCK), 0, 2) < 1).astype(jnp.int32), jax.random.fold_in(seeds[6], 1), 0, 1),
    }


def expand(mask_grid):
    return jnp.repeat(jnp.repeat(mask_grid.astype(jnp.bfloat16), BLOCK, 0), BLOCK, 1)


def reference(tokens, gate_weight, up_weight, down_weight, gate_mask, up_mask, down_mask):
    gate_kept = gate_weight * expand(gate_mask)
    up_kept = up_weight * expand(up_mask)
    down_kept = down_weight * expand(down_mask)
    feature_cols = D // N_FEAT
    gate = jnp.zeros((TOKENS, HID), jnp.float32)
    up_sum = jnp.zeros((TOKENS, HID), jnp.float32)
    for segment in range(N_FEAT):
        lower = segment * feature_cols
        inputs = tokens[:, lower:lower + feature_cols]
        gate_part = jnp.dot(inputs, gate_kept[lower:lower + feature_cols], preferred_element_type=jnp.float32)
        up_part = jnp.dot(inputs, up_kept[lower:lower + feature_cols], preferred_element_type=jnp.float32)
        gate = gate + lax.optimization_barrier(gate_part.astype(jnp.bfloat16)).astype(jnp.float32)
        up_sum = up_sum + lax.optimization_barrier(up_part.astype(jnp.bfloat16)).astype(jnp.float32)
    hidden = (jax.nn.silu(gate) * up_sum).astype(jnp.bfloat16)
    hidden_cols = HID // (N_TOK * N_REP)
    output = jnp.zeros((TOKENS, D), jnp.float32)
    for segment in range(N_TOK * N_REP):
        lower = segment * hidden_cols
        down_part = jnp.dot(hidden[:, lower:lower + hidden_cols], down_kept[lower:lower + hidden_cols], preferred_element_type=jnp.float32)
        output = output + lax.optimization_barrier(down_part.astype(jnp.bfloat16)).astype(jnp.float32)
    return output.astype(jnp.bfloat16)
```

```python
import functools

import jax
import jax.numpy as jnp
from jax import lax
from jax.experimental import pallas as pl
from jax.experimental.pallas import tpu as pltpu
from jax.sharding import PartitionSpec as P

BLOCK = 128
HOP = 2
BACK = 1
EARLY = 2
MESH = pl.DeviceIdType.MESH


def kernel(nf, nx, nr, tokens, gate_w, up_w, down_w, gate_m, up_m, down_m, out,
           arrived, tok, wgu, wd, sums, part, taken, hid, acc, leaving, coming,
           tok_send, tok_recv, own_sem, g_sem, u_sem, d_sem, part_send, part_recv,
           hid_send, hid_recv, out_send, out_recv):
    z, x, r = lax.axis_index("feat"), lax.axis_index("tok"), lax.axis_index("rep")
    rows = arrived.shape[1]
    feats = tok.shape[2]
    chunks = wgu.shape[0]
    width = wd.shape[1]
    up_chunks, down_chunks = (chunks + 1) // 2, chunks // 2
    early = min(EARLY, down_chunks)
    peers = [(g, q) for g in range(nx) for q in range(nr)]

    def chip(g):
        return lax.rem(x + 1 + g, nx)

    barrier = pltpu.get_barrier_semaphore()
    for g in range(nx - 1):
        for q in range(nr):
            pl.semaphore_signal(barrier, inc=1, device_id={"tok": chip(g), "rep": q}, device_id_type=MESH)
    for step in range(1, nr):
        pl.semaphore_signal(barrier, inc=1, device_id={"rep": lax.rem(r + step, nr)}, device_id_type=MESH)

    @pl.when(z > 0)
    def _():
        pl.semaphore_signal(barrier, inc=1, device_id={"feat": z - 1}, device_id_type=MESH)

    @pl.when(z < nf - 1)
    def _():
        pl.semaphore_signal(barrier, inc=1, device_id={"feat": z + 1}, device_id_type=MESH)

    def gate_copy(j):
        cols = pl.ds(pl.multiple_of(j * width, width), width)
        return pltpu.make_async_copy(gate_w.at[:, cols], wgu.at[j, :, pl.ds(0, width)], g_sem.at[j])

    def up_copy(j):
        cols = pl.ds(pl.multiple_of(j * width, width), width)
        return pltpu.make_async_copy(up_w.at[:, cols], wgu.at[j, :, pl.ds(width, width)], u_sem.at[j])

    def down_copy(j):
        at = pl.ds(pl.multiple_of(j * width, width), width)
        return pltpu.make_async_copy(down_w.at[at, :], wd.at[j], d_sem.at[j])

    own_copy = pltpu.make_async_copy(tokens, arrived.at[(nx - 1) * nr + r], own_sem)
    own_copy.start()
    for c in range(up_chunks):
        for j in ([c, up_chunks + c] if c < down_chunks else [c]):
            gate_copy(j).start()
            up_copy(j).start()
    for c in range(up_chunks):
        for j in ([c, up_chunks + c] if c < down_chunks else [c]):
            down_copy(j).start()
    acc[...] = jnp.zeros_like(acc)

    ends = (z == 0).astype(jnp.int32) + (z == nf - 1).astype(jnp.int32)
    pl.semaphore_wait(barrier, nx * nr + 1 - ends)

    def near_copy(step):
        return pltpu.make_async_remote_copy(
            src_ref=tokens, dst_ref=arrived.at[(nx - 1) * nr + r],
            send_sem=tok_send.at[(nx - 1) * nr + step], recv_sem=tok_recv.at[(nx - 1) * nr + r],
            device_id={"rep": lax.rem(r + step, nr)}, device_id_type=MESH)

    def far_copy(g, q):
        slot = (nx - 2 - g) * nr + r
        return pltpu.make_async_remote_copy(
            src_ref=tokens, dst_ref=arrived.at[slot],
            send_sem=tok_send.at[g * nr + q], recv_sem=tok_recv.at[slot],
            device_id={"tok": chip(g), "rep": q}, device_id_type=MESH)

    def landed(slot):
        pltpu.make_async_remote_copy(
            src_ref=tokens, dst_ref=arrived.at[slot],
            send_sem=tok_send.at[0], recv_sem=tok_recv.at[slot],
            device_id={"rep": lax.rem(r + 1, nr)}, device_id_type=MESH).wait_recv()

    for step in range(1, nr):
        near_copy(step).start()
    for g in range(nx - 1):
        for q in range(nr):
            far_copy(g, q).start()
    own_copy.wait()
    for step in range(1, nr):
        landed((nx - 1) * nr + lax.rem(r + step, nr))
    for q in range(nr):
        tok[nx - 1, q * rows:(q + 1) * rows, :] = arrived[(nx - 1) * nr + q]

    def place(d):
        p = jnp.where(d == 0, z, nf - 1 - z)
        count = up_chunks if up_chunks == down_chunks else jnp.where(d == 0, up_chunks, down_chunks)
        return p, count, nx * count

    def unit(u, d, count):
        mine = (u < early) | (u >= early + (nx - 1) * count)
        other = jnp.maximum(u - early, 0)
        group = jnp.where(mine, nx - 1, other // count)
        c = jnp.where(u < early, u, jnp.where(mine, u - (nx - 1) * count, other % count))
        first = (u < early) | ((u >= 2 * early) & (u < early + count))
        return group, d * up_chunks + c, first

    def ahead(d):
        return z + 1 - 2 * d

    def behind(d):
        return z - 1 + 2 * d

    def part_copy(d, u):
        return pltpu.make_async_remote_copy(
            src_ref=part.at[d, u], dst_ref=taken.at[d, u],
            send_sem=part_send.at[d, u], recv_sem=part_recv.at[d, u],
            device_id={"feat": ahead(d)}, device_id_type=MESH)

    def hid_copy(d, u):
        return pltpu.make_async_remote_copy(
            src_ref=hid.at[d, u], dst_ref=hid.at[d, u],
            send_sem=hid_send.at[d, u], recv_sem=hid_recv.at[d, u],
            device_id={"feat": behind(d)}, device_id_type=MESH)

    def splat(scalar, shape):
        return jnp.full(shape, scalar.astype(jnp.float32)).astype(jnp.bfloat16)

    def first_half(i, d):
        p, count, units = place(d)
        u = i - HOP * p

        @pl.when((u >= 0) & (u < units))
        def _():
            group, j, first = unit(u, d, count)

            @pl.when(first)
            def _():
                gate_copy(j).wait()
                up_copy(j).wait()

            total = None
            deep = 2 * BLOCK if feats % (2 * BLOCK) == 0 else BLOCK
            for lo in range(0, feats, deep):
                tall = []
                for b in range(lo // BLOCK, (lo + deep) // BLOCK):
                    wide = []
                    for n in range(2 * width // BLOCK):
                        mask = gate_m if n < width // BLOCK else up_m
                        keep = mask[b, j * (width // BLOCK) + n % (width // BLOCK)]
                        wide.append(wgu[j, b * BLOCK:(b + 1) * BLOCK, n * BLOCK:(n + 1) * BLOCK] * splat(keep, (BLOCK, BLOCK)))
                    tall.append(jnp.concatenate(wide, axis=1))
                product = jnp.dot(tok[group, :, lo:lo + deep], jnp.concatenate(tall, axis=0),
                                  preferred_element_type=jnp.float32)
                total = product if total is None else total + product
            sums[...] = total

            @pl.when(p > 0)
            def _():
                part_copy(d, u).wait_recv()
                sums[...] += taken[d, u].astype(jnp.float32)

            @pl.when(p < nf - 1)
            def _():
                part[d, u] = sums[...].astype(jnp.bfloat16)
                part_copy(d, u).start()

            @pl.when(p == nf - 1)
            def _():
                gate, up = sums[:, :width], sums[:, width:]
                hid[d, u] = (gate / (1.0 + jnp.exp(-gate)) * up).astype(jnp.bfloat16)
                hid_copy(d, u).start()

    def second_half(i, d):
        p, count, units = place(d)
        h = i - HOP * (nf - 1) - BACK * (nf - 1 - p)

        @pl.when((h >= 0) & (h < units))
        def _():
            group, j, first = unit(h, d, count)

            @pl.when(p < nf - 1)
            def _():
                hid_copy(d, h).wait_recv()

                @pl.when(p > 0)
                def _():
                    hid_copy(d, h).start()

            @pl.when(first)
            def _():
                down_copy(j).wait()

            for n in range(wd.shape[2] // BLOCK // 2):
                cols = slice(2 * n * BLOCK, 2 * (n + 1) * BLOCK)
                tall = []
                for b in range(width // BLOCK):
                    wide = []
                    for m in (2 * n, 2 * n + 1):
                        keep = down_m[j * (width // BLOCK) + b, m]
                        wide.append(wd[j, b * BLOCK:(b + 1) * BLOCK, m * BLOCK:(m + 1) * BLOCK] * splat(keep, (BLOCK, BLOCK)))
                    tall.append(jnp.concatenate(wide, axis=1))
                acc[group, :, cols] += jnp.dot(hid[d, h], jnp.concatenate(tall, axis=0),
                                               preferred_element_type=jnp.float32)

    def out_copy(g, q):
        slot = g * nr + r
        return pltpu.make_async_remote_copy(
            src_ref=leaving.at[g * nr + q], dst_ref=coming.at[slot],
            send_sem=out_send.at[g * nr + q], recv_sem=out_recv.at[slot],
            device_id={"tok": chip(g), "rep": q}, device_id_type=MESH)

    def last_copy(step):
        return pltpu.make_async_remote_copy(
            src_ref=leaving.at[(nx - 1) * nr + step], dst_ref=coming.at[(nx - 1) * nr + r],
            send_sem=out_send.at[(nx - 1) * nr + step], recv_sem=out_recv.at[(nx - 1) * nr + r],
            device_id={"rep": lax.rem(r + step, nr)}, device_id_type=MESH)

    starts = HOP * jnp.minimum(z, nf - 1 - z) + early

    @pl.loop(0, nx * up_chunks + (HOP + BACK) * (nf - 1))
    def _(i):
        @pl.when(i == starts)
        def _():
            for g in range(nx - 1):
                for q in range(nr):
                    landed(g * nr + q)
                    tok[g, q * rows:(q + 1) * rows, :] = arrived[g * nr + q]

        @pl.loop(0, 2)
        def _(d):
            first_half(i, d)

        @pl.loop(0, 2)
        def _(d):
            second_half(i, d)

        for g in range(nx - 1):
            ends = [early + (g + 1) * count - 1 + HOP * (nf - 1) + BACK * (nf - 1 - p)
                    for count, p in ((up_chunks, z), (down_chunks, nf - 1 - z))]

            @pl.when(i == jnp.maximum(*ends))
            def _():
                for q in range(nr):
                    leaving[g * nr + q] = acc[g, q * rows:(q + 1) * rows, :].astype(jnp.bfloat16)
                    out_copy(g, q).start()

    for step in range(1, nr):
        at = pl.ds(pl.multiple_of(lax.rem(r + step, nr) * rows, 8), rows)
        leaving[(nx - 1) * nr + step] = acc[nx - 1, at, :].astype(jnp.bfloat16)
        last_copy(step).start()
    final = acc[nx - 1, pl.ds(pl.multiple_of(r * rows, 8), rows), :]

    def summed(slot):
        pltpu.make_async_remote_copy(
            src_ref=leaving.at[0], dst_ref=coming.at[slot],
            send_sem=out_send.at[0], recv_sem=out_recv.at[slot],
            device_id={"rep": lax.rem(r + 1, nr)}, device_id_type=MESH).wait_recv()
        return coming[slot].astype(jnp.float32)

    for slot in range((nx - 1) * nr):
        final += summed(slot)
    for step in range(1, nr):
        final += summed((nx - 1) * nr + lax.rem(r + step, nr))
    out[...] = final.astype(out.dtype)

    for step in range(1, nr):
        near_copy(step).wait_send()
        last_copy(step).wait_send()
    for g in range(nx - 1):
        for q in range(nr):
            far_copy(g, q).wait_send()
            out_copy(g, q).wait_send()

    @pl.loop(0, 2)
    def _(d):
        p, count, units = place(d)

        @pl.loop(0, nx * up_chunks)
        def _(u):
            @pl.when((u < units) & (p < nf - 1))
            def _():
                part_copy(d, u).wait_send()

            @pl.when((u < units) & (p > 0))
            def _():
                hid_copy(d, u).wait_send()


def solution(mesh):
    nf, nx, nr = mesh.shape["feat"], mesh.shape["tok"], mesh.shape["rep"]

    def shards(tokens, gate_weight, up_weight, down_weight, gate_mask, up_mask, down_mask):
        rows, feats = tokens.shape
        hidden = gate_weight.shape[1]
        width = 2 * BLOCK if hidden % (4 * BLOCK) == 0 else BLOCK
        chunks = hidden // width
        units = nx * ((chunks + 1) // 2)
        high = nr * rows
        bf16, f32 = jnp.bfloat16, jnp.float32
        dma = pltpu.SemaphoreType.DMA
        hbm, smem = pl.BlockSpec(memory_space=pl.ANY), pl.BlockSpec(memory_space=pltpu.SMEM)
        return pl.pallas_call(
            functools.partial(kernel, nf, nx, nr),
            out_shape=jax.ShapeDtypeStruct((rows, feats), bf16),
            in_specs=[hbm] * 4 + [smem] * 3,
            out_specs=pl.BlockSpec(memory_space=pltpu.VMEM),
            scratch_shapes=[
                pltpu.VMEM((nx * nr, rows, feats), bf16),
                pltpu.VMEM((nx, high, feats), bf16),
                pltpu.VMEM((chunks, feats, 2 * width), bf16),
                pltpu.VMEM((chunks, width, feats), bf16),
                pltpu.VMEM((high, 2 * width), f32),
                pltpu.VMEM((2, units, high, 2 * width), bf16),
                pltpu.VMEM((2, units, high, 2 * width), bf16),
                pltpu.VMEM((2, units, high, width), bf16),
                pltpu.VMEM((nx, high, feats), f32),
                pltpu.VMEM((nx * nr, rows, feats), bf16),
                pltpu.VMEM((nx * nr, rows, feats), bf16),
                dma((nx * nr,)), dma((nx * nr,)), dma(()),
                dma((chunks,)), dma((chunks,)), dma((chunks,)),
                dma((2, units)), dma((2, units)), dma((2, units)), dma((2, units)),
                dma((nx * nr,)), dma((nx * nr,)),
            ],
            compiler_params=pltpu.CompilerParams(
                collective_id=0, has_side_effects=True, vmem_limit_bytes=63 * 1024 * 1024),
        )(tokens, gate_weight, up_weight, down_weight, gate_mask, up_mask, down_mask)

    return jax.shard_map(
        shards,
        mesh=mesh,
        in_specs=(
            P(("groups", "tok", "rep"), "feat"),
            P("feat", ("tok", "rep")),
            P("feat", ("tok", "rep")),
            P(("tok", "rep"), "feat"),
            P("feat", ("tok", "rep")),
            P("feat", ("tok", "rep")),
            P(("tok", "rep"), "feat"),
        ),
        out_specs=P(("groups", "tok", "rep"), "feat"),
        check_vma=False,
    )
```

```python
import functools

import jax
import jax.numpy as jnp
from jax import lax
from jax.experimental import pallas as pl
from jax.experimental.pallas import tpu as pltpu
from jax.sharding import PartitionSpec as P

BLOCK = 128
HOP = 2
BACK = 2
LEAD = 2
DELAY = 3
EARLY = 2
MESH = pl.DeviceIdType.MESH


def kernel(nf, nx, nr, tokens, gate_w, up_w, down_w, gate_m, up_m, down_m, out,
           arrived, tok, wgu, wd, sums, part, taken, hid, acc, leaving, coming,
           tok_send, tok_recv, own_sem, g_sem, u_sem, d_sem, part_send, part_recv,
           hid_send, hid_recv, out_send, out_recv):
    z, x, r = lax.axis_index("feat"), lax.axis_index("tok"), lax.axis_index("rep")
    rows = arrived.shape[1]
    feats = tok.shape[2]
    chunks = wgu.shape[0]
    width = wd.shape[1]
    up_chunks, down_chunks = (chunks + 1) // 2, chunks // 2
    early = min(EARLY, down_chunks)
    peers = [(g, q) for g in range(nx) for q in range(nr)]

    def chip(g):
        return lax.rem(x + 1 + g, nx)

    barrier = pltpu.get_barrier_semaphore()
    for g in range(nx - 1):
        for q in range(nr):
            pl.semaphore_signal(barrier, inc=1, device_id={"tok": chip(g), "rep": q}, device_id_type=MESH)
    for step in range(1, nr):
        pl.semaphore_signal(barrier, inc=1, device_id={"rep": lax.rem(r + step, nr)}, device_id_type=MESH)

    @pl.when(z > 0)
    def _():
        pl.semaphore_signal(barrier, inc=1, device_id={"feat": z - 1}, device_id_type=MESH)

    @pl.when(z < nf - 1)
    def _():
        pl.semaphore_signal(barrier, inc=1, device_id={"feat": z + 1}, device_id_type=MESH)

    def gate_copy(j):
        cols = pl.ds(pl.multiple_of(j * width, width), width)
        return pltpu.make_async_copy(gate_w.at[:, cols], wgu.at[j, :, pl.ds(0, width)], g_sem.at[j])

    def up_copy(j):
        cols = pl.ds(pl.multiple_of(j * width, width), width)
        return pltpu.make_async_copy(up_w.at[:, cols], wgu.at[j, :, pl.ds(width, width)], u_sem.at[j])

    def down_copy(j):
        at = pl.ds(pl.multiple_of(j * width, width), width)
        return pltpu.make_async_copy(down_w.at[at, :], wd.at[j], d_sem.at[j])

    own_copy = pltpu.make_async_copy(tokens, arrived.at[(nx - 1) * nr + r], own_sem)
    own_copy.start()

    def fetch(c, make):
        make(c).start()
        if up_chunks == down_chunks:
            make(up_chunks + c).start()
        else:
            @pl.when(c < down_chunks)
            def _():
                make(up_chunks + c).start()

    lead = min(LEAD, up_chunks)
    for c in range(lead):
        fetch(jnp.int32(c), gate_copy)
        fetch(jnp.int32(c), up_copy)
    acc[...] = jnp.zeros_like(acc)

    ends = (z == 0).astype(jnp.int32) + (z == nf - 1).astype(jnp.int32)
    pl.semaphore_wait(barrier, nx * nr + 1 - ends)

    def near_copy(step):
        return pltpu.make_async_remote_copy(
            src_ref=tokens, dst_ref=arrived.at[(nx - 1) * nr + r],
            send_sem=tok_send.at[(nx - 1) * nr + step], recv_sem=tok_recv.at[(nx - 1) * nr + r],
            device_id={"rep": lax.rem(r + step, nr)}, device_id_type=MESH)

    def far_copy(g, q):
        slot = (nx - 2 - g) * nr + r
        return pltpu.make_async_remote_copy(
            src_ref=tokens, dst_ref=arrived.at[slot],
            send_sem=tok_send.at[g * nr + q], recv_sem=tok_recv.at[slot],
            device_id={"tok": chip(g), "rep": q}, device_id_type=MESH)

    def landed(slot):
        pltpu.make_async_remote_copy(
            src_ref=tokens, dst_ref=arrived.at[slot],
            send_sem=tok_send.at[0], recv_sem=tok_recv.at[slot],
            device_id={"rep": lax.rem(r + 1, nr)}, device_id_type=MESH).wait_recv()

    for step in range(1, nr):
        near_copy(step).start()
    for g in range(nx - 1):
        for q in range(nr):
            far_copy(g, q).start()
    own_copy.wait()
    for step in range(1, nr):
        landed((nx - 1) * nr + lax.rem(r + step, nr))
    for q in range(nr):
        tok[nx - 1, q * rows:(q + 1) * rows, :] = arrived[(nx - 1) * nr + q]

    def place(d):
        p = jnp.where(d == 0, z, nf - 1 - z)
        count = up_chunks if up_chunks == down_chunks else jnp.where(d == 0, up_chunks, down_chunks)
        return p, count, nx * count

    def unit(u, d, count):
        mine = (u < early) | (u >= early + (nx - 1) * count)
        other = jnp.maximum(u - early, 0)
        group = jnp.where(mine, nx - 1, other // count)
        c = jnp.where(u < early, u, jnp.where(mine, u - (nx - 1) * count, other % count))
        first = (u < early) | ((u >= 2 * early) & (u < early + count))
        return group, d * up_chunks + c, first

    def ahead(d):
        return z + 1 - 2 * d

    def behind(d):
        return z - 1 + 2 * d

    def part_copy(d, u):
        return pltpu.make_async_remote_copy(
            src_ref=part.at[d, u], dst_ref=taken.at[d, u],
            send_sem=part_send.at[d, u], recv_sem=part_recv.at[d, u],
            device_id={"feat": ahead(d)}, device_id_type=MESH)

    def hid_copy(d, u):
        return pltpu.make_async_remote_copy(
            src_ref=hid.at[d, u], dst_ref=hid.at[d, u],
            send_sem=hid_send.at[d, u], recv_sem=hid_recv.at[d, u],
            device_id={"feat": behind(d)}, device_id_type=MESH)

    def splat(scalar, shape):
        return jnp.full(shape, scalar.astype(jnp.float32)).astype(jnp.bfloat16)

    def first_half(i, d):
        p, count, units = place(d)
        u = i - HOP * p

        @pl.when((u >= 0) & (u < units))
        def _():
            group, j, first = unit(u, d, count)

            @pl.when(first)
            def _():
                gate_copy(j).wait()
                up_copy(j).wait()

            total = None
            deep = 2 * BLOCK if feats % (2 * BLOCK) == 0 else BLOCK
            for lo in range(0, feats, deep):
                tall = []
                for b in range(lo // BLOCK, (lo + deep) // BLOCK):
                    wide = []
                    for n in range(2 * width // BLOCK):
                        mask = gate_m if n < width // BLOCK else up_m
                        keep = mask[b, j * (width // BLOCK) + n % (width // BLOCK)]
                        wide.append(wgu[j, b * BLOCK:(b + 1) * BLOCK, n * BLOCK:(n + 1) * BLOCK] * splat(keep, (BLOCK, BLOCK)))
                    tall.append(jnp.concatenate(wide, axis=1))
                product = jnp.dot(tok[group, :, lo:lo + deep], jnp.concatenate(tall, axis=0),
                                  preferred_element_type=jnp.float32)
                total = product if total is None else total + product
            sums[...] = total

            @pl.when(p > 0)
            def _():
                part_copy(d, u).wait_recv()
                sums[...] += taken[d, u].astype(jnp.float32)

            @pl.when(p < nf - 1)
            def _():
                part[d, u] = sums[...].astype(jnp.bfloat16)
                part_copy(d, u).start()

            @pl.when(p == nf - 1)
            def _():
                gate, up = sums[:, :width], sums[:, width:]
                hid[d, u] = (gate / (1.0 + jnp.exp(-gate)) * up).astype(jnp.bfloat16)

    def second_half(i, d):
        p, count, units = place(d)
        h = i - HOP * (nf - 1) - DELAY - BACK * (nf - 1 - p)

        @pl.when((h >= 0) & (h < units))
        def _():
            group, j, first = unit(h, d, count)

            @pl.when(p < nf - 1)
            def _():
                hid_copy(d, h).wait_recv()

            @pl.when(p > 0)
            def _():
                hid_copy(d, h).start()

            @pl.when(first)
            def _():
                down_copy(j).wait()

            for n in range(wd.shape[2] // BLOCK // 2):
                cols = slice(2 * n * BLOCK, 2 * (n + 1) * BLOCK)
                tall = []
                for b in range(width // BLOCK):
                    wide = []
                    for m in (2 * n, 2 * n + 1):
                        keep = down_m[m, j * (width // BLOCK) + b]
                        wide.append(wd[j, b * BLOCK:(b + 1) * BLOCK, m * BLOCK:(m + 1) * BLOCK] * splat(keep, (BLOCK, BLOCK)))
                    tall.append(jnp.concatenate(wide, axis=1))
                acc[group, :, cols] += jnp.dot(hid[d, h], jnp.concatenate(tall, axis=0),
                                               preferred_element_type=jnp.float32)

    def out_copy(g, q):
        slot = g * nr + r
        return pltpu.make_async_remote_copy(
            src_ref=leaving.at[g * nr + q], dst_ref=coming.at[slot],
            send_sem=out_send.at[g * nr + q], recv_sem=out_recv.at[slot],
            device_id={"tok": chip(g), "rep": q}, device_id_type=MESH)

    def last_copy(step):
        return pltpu.make_async_remote_copy(
            src_ref=leaving.at[(nx - 1) * nr + step], dst_ref=coming.at[(nx - 1) * nr + r],
            send_sem=out_send.at[(nx - 1) * nr + step], recv_sem=out_recv.at[(nx - 1) * nr + r],
            device_id={"rep": lax.rem(r + step, nr)}, device_id_type=MESH)

    starts = HOP * jnp.minimum(z, nf - 1 - z) + early

    @pl.loop(0, nx * up_chunks + (HOP + BACK) * (nf - 1) + DELAY)
    def _(i):
        @pl.when(i == starts)
        def _():
            for g in range(nx - 1):
                for q in range(nr):
                    landed(g * nr + q)
                    tok[g, q * rows:(q + 1) * rows, :] = arrived[g * nr + q]

        @pl.when(i + lead < up_chunks)
        def _():
            fetch(i + lead, gate_copy)
            fetch(i + lead, up_copy)

        @pl.when(i < up_chunks)
        def _():
            fetch(i, down_copy)

        @pl.loop(0, 2)
        def _(d):
            first_half(i, d)

        @pl.loop(0, 2)
        def _(d):
            second_half(i, d)

        for g in range(nx - 1):
            ends = [early + (g + 1) * count - 1 + HOP * (nf - 1) + DELAY + BACK * (nf - 1 - p)
                    for count, p in ((up_chunks, z), (down_chunks, nf - 1 - z))]

            @pl.when(i == jnp.maximum(*ends))
            def _():
                for q in range(nr):
                    leaving[g * nr + q] = acc[g, q * rows:(q + 1) * rows, :].astype(jnp.bfloat16)
                    out_copy(g, q).start()

    for step in range(1, nr):
        at = pl.ds(pl.multiple_of(lax.rem(r + step, nr) * rows, 8), rows)
        leaving[(nx - 1) * nr + step] = acc[nx - 1, at, :].astype(jnp.bfloat16)
        last_copy(step).start()
    final = acc[nx - 1, pl.ds(pl.multiple_of(r * rows, 8), rows), :]

    def summed(slot):
        pltpu.make_async_remote_copy(
            src_ref=leaving.at[0], dst_ref=coming.at[slot],
            send_sem=out_send.at[0], recv_sem=out_recv.at[slot],
            device_id={"rep": lax.rem(r + 1, nr)}, device_id_type=MESH).wait_recv()
        return coming[slot].astype(jnp.float32)

    for slot in range((nx - 1) * nr):
        final += summed(slot)
    for step in range(1, nr):
        final += summed((nx - 1) * nr + lax.rem(r + step, nr))
    out[...] = final.astype(out.dtype)

    for step in range(1, nr):
        near_copy(step).wait_send()
        last_copy(step).wait_send()
    for g in range(nx - 1):
        for q in range(nr):
            far_copy(g, q).wait_send()
            out_copy(g, q).wait_send()

    @pl.loop(0, 2)
    def _(d):
        p, count, units = place(d)

        @pl.loop(0, nx * up_chunks)
        def _(u):
            @pl.when((u < units) & (p < nf - 1))
            def _():
                part_copy(d, u).wait_send()

            @pl.when((u < units) & (p > 0))
            def _():
                hid_copy(d, u).wait_send()


def solution(mesh):
    nf, nx, nr = mesh.shape["feat"], mesh.shape["tok"], mesh.shape["rep"]

    def shards(tokens, gate_weight, up_weight, down_weight, gate_mask, up_mask, down_mask):
        rows, feats = tokens.shape
        hidden = gate_weight.shape[1]
        width = 2 * BLOCK if hidden % (4 * BLOCK) == 0 else BLOCK
        chunks = hidden // width
        units = nx * ((chunks + 1) // 2)
        high = nr * rows
        bf16, f32 = jnp.bfloat16, jnp.float32
        dma = pltpu.SemaphoreType.DMA
        hbm, smem = pl.BlockSpec(memory_space=pl.ANY), pl.BlockSpec(memory_space=pltpu.SMEM)
        return pl.pallas_call(
            functools.partial(kernel, nf, nx, nr),
            out_shape=jax.ShapeDtypeStruct((rows, feats), bf16),
            in_specs=[hbm] * 4 + [smem] * 3,
            out_specs=pl.BlockSpec(memory_space=pltpu.VMEM),
            scratch_shapes=[
                pltpu.VMEM((nx * nr, rows, feats), bf16),
                pltpu.VMEM((nx, high, feats), bf16),
                pltpu.VMEM((chunks, feats, 2 * width), bf16),
                pltpu.VMEM((chunks, width, feats), bf16),
                pltpu.VMEM((high, 2 * width), f32),
                pltpu.VMEM((2, units, high, 2 * width), bf16),
                pltpu.VMEM((2, units, high, 2 * width), bf16),
                pltpu.VMEM((2, units, high, width), bf16),
                pltpu.VMEM((nx, high, feats), f32),
                pltpu.VMEM((nx * nr, rows, feats), bf16),
                pltpu.VMEM((nx * nr, rows, feats), bf16),
                dma((nx * nr,)), dma((nx * nr,)), dma(()),
                dma((chunks,)), dma((chunks,)), dma((chunks,)),
                dma((2, units)), dma((2, units)), dma((2, units)), dma((2, units)),
                dma((nx * nr,)), dma((nx * nr,)),
            ],
            compiler_params=pltpu.CompilerParams(
                collective_id=0, has_side_effects=True, vmem_limit_bytes=63 * 1024 * 1024),
        )(tokens, gate_weight, up_weight, down_weight, gate_mask, up_mask, down_mask.T)

    return jax.shard_map(
        shards,
        mesh=mesh,
        in_specs=(
            P(("groups", "tok", "rep"), "feat"),
            P("feat", ("tok", "rep")),
            P("feat", ("tok", "rep")),
            P(("tok", "rep"), "feat"),
            P("feat", ("tok", "rep")),
            P("feat", ("tok", "rep")),
            P(("tok", "rep"), "feat"),
        ),
        out_specs=P(("groups", "tok", "rep"), "feat"),
        check_vma=False,
    )
```
